128 devices in a mesh: section: 8 (over z_hi, y), seq: 8 (over x, z_lo), mp: 2 (over core).
Axes of the slice: x: 4, y: 4, z: 4 (z_hi: 2, z_lo: 2; z = z_hi * 2 + z_lo), core: 2. Of those that a mesh axis runs over, the one named last changes fastest.
Arguments:
- resid: bfloat16 [8, 2048, 4096], P('section', 'seq', 'mp'), may hold values from -3 to 3
- span_q: bfloat16 [8, 2048, 4096], P('section', 'seq', 'mp'), may hold values from -6 to 6
- span_k: bfloat16 [8, 2048, 4096], P('section', 'seq', 'mp'), may hold values from -6 to 6
- span_v: bfloat16 [8, 2048, 4096], P('section', 'seq', 'mp'), may hold values from -6 to 6
- cache_k: bfloat16 [4, 2048, 4096], P(None, 'seq', 'mp'), may hold values from -6 to 6
- cache_v: bfloat16 [4, 2048, 4096], P(None, 'seq', 'mp'), may hold values from -6 to 6
- cache_index: int32 [8], P('section'), may hold values from 0 to 3
- tile_mask: int32 [8, 16, 48], P('section'), may hold values from 0 to 1, as said below
Outputs:
- updated: bfloat16 [8, 2048, 4096], P('section', 'seq', 'mp')
The draws below stay inside these ranges and needn't reach their ends.
Inputs may be any that keep to these rules, and one draw needn't show every extreme that they name: tile_mask[s, i, i] is 1 for every group s and query tile i: every query tile sees its own key tile.
All inputs are finite; a program needn't handle non-finite values.
Results may differ from the reference program's by a relative error of at most 0.0044.
Values may be sent and summed in bfloat16 or wider, within the bound.
A program may use at most 320 MiB of HBM per device.

```python
import jax
import jax.numpy as jnp
from jax import lax

HEADS = 32
HD = 128
TILE = 128
CACHE = 4
SECTIONS = 8
SPAN = 2048
F = 4096
QT = 16
KT = 48


def draw_span_q(key, part):
    own_key = jax.random.fold_in(key, 1)
    shape = (SECTIONS, SPAN, F)
    base = jnp.clip(1.6 * jax.random.normal(own_key, shape, jnp.float32), -6.0, 6.0)
    return base.astype(jnp.bfloat16)


def draw_span_k(key, part):
    own_key = jax.random.fold_in(key, 2)
    shape = (SECTIONS, SPAN, F)
    base = jnp.clip(1.6 * jax.random.normal(own_key, shape, jnp.float32), -6.0, 6.0)
    return base.astype(jnp.bfloat16)


def draw_tile_mask(key, part):
    rate_key = jax.random.fold_in(key, 3)
    pick_key = jax.random.fold_in(key, 4)
    rates = jax.random.randint(rate_key, (SECTIONS, QT, 1), 10, 70)
    picks = jax.random.randint(pick_key, (SECTIONS, QT, KT), 0, 100)
    query_ids = jnp.arange(QT)[None, :, None]
    key_ids = jnp.arange(KT)[None, None, :]
    allowed = (picks < rates) | (query_ids == key_ids)
    return allowed.astype(jnp.int32)


def touch_ends(result, key, low, largest):
    place = [jax.random.randint(jax.random.fold_in(key, axis), (), 0, length) for axis, length in enumerate(result.shape)]
    longest = result.shape.index(max(result.shape))
    next_to = place[:longest] + [(place[longest] + 1) % result.shape[longest]] + place[longest + 1:]
    return result.at[tuple(place)].set(low).at[tuple(next_to)].set(largest)


def block_scale(stream_key, shape, shards, smallest, high):
    gain, own = 1.0, jax.random.fold_in(stream_key, 6)
    for position, parts in shards:
        draws = jnp.exp(jax.random.uniform(jax.random.fold_in(own, position), (parts,), jnp.float32, smallest / len(shards), high / len(shards)))
        gain = gain * jnp.repeat(draws, shape[position] // parts).reshape([-1 if axis == position else 1 for axis in range(len(shape))])
    return gain


def noise(key, dims, deviation, bound, cuts=(), kind=jnp.bfloat16):
    entries = deviation * jax.random.normal(key, dims, jnp.float32)
    if cuts:
        entries = entries * block_scale(key, dims, cuts, -0.22, 0.18)
    return jnp.clip(entries, -bound, bound).astype(kind)


def setup_inputs(seed: int = 0) -> dict:
    seeds = jax.random.split(jax.random.key(seed), 9)
    resid = noise(seeds[0], (SECTIONS, SPAN, F), 0.5, 3.0, ((0, 8), (1, 8), (2, 2)))
    span_q = draw_span_q(jax.random.fold_in(seeds[8], 71), 0)
    span_k = draw_span_k(jax.random.fold_in(seeds[8], 71), 0)
    span_v = noise(seeds[3], (SECTIONS, SPAN, F), 1.0, 6.0, ((0, 8), (1, 8), (2, 2)))
    cache_k = noise(seeds[4], (CACHE, SPAN, F), 1.6, 6.0, ((1, 8), (2, 2)))
    cache_v = noise(seeds[5], (CACHE, SPAN, F), 1.0, 6.0, ((1, 8), (2, 2)))
    cache_index = touch_ends(jax.random.randint(seeds[6], (SECTIONS,), 0, CACHE), jax.random.fold_in(seeds[6], 1), 0, CACHE - 1).astype(jnp.int32)
    tile_mask = draw_tile_mask(jax.random.fold_in(seeds[8], 71), 0)
    return {"resid": resid, "span_q": span_q, "span_k": span_k, "span_v": span_v, "cache_k": cache_k, "cache_v": cache_v, "cache_index": cache_index, "tile_mask": tile_mask}


def one_section(section_id, span_q, span_k, span_v, cache_k, cache_v, cache_index, tile_mask):
    fresh_k = span_k[SECTIONS - 1]
    fresh_v = span_v[SECTIONS - 1]
    queries = lax.dynamic_index_in_dim(span_q, section_id, 0, keepdims=False)
    own_k = lax.dynamic_index_in_dim(span_k, section_id, 0, keepdims=False)
    own_v = lax.dynamic_index_in_dim(span_v, section_id, 0, keepdims=False)
    block = lax.dynamic_index_in_dim(cache_index, section_id, 0, keepdims=False).astype(jnp.int32)
    cached_k = lax.dynamic_index_in_dim(cache_k, block, 0, keepdims=False)
    cached_v = lax.dynamic_index_in_dim(cache_v, block, 0, keepdims=False)
    keys = jnp.concatenate([own_k, fresh_k, cached_k], 0)
    values = jnp.concatenate([own_v, fresh_v, cached_v], 0)
    masks = lax.dynamic_index_in_dim(tile_mask, section_id, 0, keepdims=False)
    query_tiles = jnp.arange(SPAN) // TILE
    key_tiles = jnp.arange(3 * SPAN) // TILE
    allowed = masks[query_tiles][:, key_tiles] > 0
    scale = 1.0 / (HD ** 0.5)

    def one_head(head):
        start = (head * HD).astype(jnp.int32)
        q_head = lax.dynamic_slice_in_dim(queries, start, HD, 1)
        k_head = lax.dynamic_slice_in_dim(keys, start, HD, 1)
        v_head = lax.dynamic_slice_in_dim(values, start, HD, 1)
        score = jnp.dot(q_head, k_head.T, preferred_element_type=jnp.float32) * scale
        masked = jnp.where(allowed, score, -1e30)
        top = jnp.max(masked, axis=1, keepdims=True)
        expo = jnp.where(allowed, jnp.exp(masked - top), 0.0)
        total = jnp.sum(expo, axis=1, keepdims=True)
        weight = expo.astype(jnp.bfloat16)
        return jnp.dot(weight, v_head, preferred_element_type=jnp.float32) / total

    heads_out = lax.map(one_head, jnp.arange(HEADS, dtype=jnp.int32))
    return jnp.transpose(heads_out, (1, 0, 2)).reshape(SPAN, F).astype(jnp.bfloat16)


def reference(resid, span_q, span_k, span_v, cache_k, cache_v, cache_index, tile_mask):
    def section_fn(section_id):
        return one_section(section_id, span_q, span_k, span_v, cache_k, cache_v, cache_index, tile_mask)

    attn = lax.map(section_fn, jnp.arange(SECTIONS, dtype=jnp.int32))
    attn = lax.optimization_barrier(attn)
    incoming = jnp.concatenate([jnp.zeros((1, SPAN, F), jnp.float32), resid[:-1].astype(jnp.float32)], 0)
    return (incoming + attn.astype(jnp.float32)).astype(jnp.bfloat16)
```

```python
import functools
import math

import jax
import jax.numpy as jnp
from jax import lax
from jax.experimental import pallas as pl
from jax.experimental.pallas import tpu as pltpu
from jax.sharding import PartitionSpec as P

HD = 128
TILE = 128
MESH = pl.DeviceIdType.MESH
HBM = pl.BlockSpec(memory_space=pl.ANY)
VMEM = pl.BlockSpec(memory_space=pltpu.VMEM)
F32 = jnp.float32
BF16 = jnp.bfloat16
RATE = math.log2(math.e) / math.sqrt(HD)
OTHERS = ((2, 1), (1, 1), (3, 1), (2, 0), (0, 1), (1, 0), (3, 0))


def place():
    section, seq = lax.axis_index("section"), lax.axis_index("seq")
    return section // 4, lax.rem(section, 4), seq // 2, lax.rem(seq, 2)


def device(hi, y, x, lo):
    return {"section": hi * 4 + y, "seq": x * 2 + lo}


def head_slice(hi, x, lo):
    return 2 * x + lo + (1 - hi) * (1 - 2 * lo)


def other(step):
    hi, y, x, lo = place()
    return hi, y, lax.rem(x + step[0], 4), lax.rem(lo + step[1], 2)


TREES = (
    {7: ("up",), 4: ("up", "cross"), 5: ("up",), 0: ("up", "down"), 3: ("down",)},
    {7: ("down", "cross"), 6: ("down", "cross"), 3: ("up",), 5: ("down", "cross")},
)
PIECES = 4
LOW = -1e30
Q, K, V, CK, CV = range(5)


def fused_kernel(
    span, q, k, v, ck, cv, resid, bias, attn, inc,
    qb, kb, vb, ob, score_a, score_b, top, total, acc,
    sends, arrivals, shifts, fresh, relay_sends, out_sends, out_arrivals,
):
    hi, y, x, lo = place()
    section, seq = lax.axis_index("section"), lax.axis_index("seq")
    rows, block, part_rows = span // 8, span // 2, span // PIECES
    near = {
        "up": device(hi, lax.rem(y + 1, 4), x, lo),
        "down": device(hi, lax.rem(y + 3, 4), x, lo),
        "cross": device(1 - hi, y, x, 1 - lo),
    }
    following = {"section": lax.rem(section + 1, 8)}
    barrier = pltpu.get_barrier_semaphore()
    greeted = [device(*other(step)) for step in OTHERS] + list(near.values())
    greeted += [following, {"section": lax.rem(section + 7, 8)}]
    for target in greeted:
        pl.semaphore_signal(barrier, inc=1, device_id=target, device_id_type=MESH)
    pl.semaphore_wait(barrier, len(greeted))

    mine = head_slice(hi, x, lo)
    source = {Q: q, K: k, V: v, CK: ck, CV: cv}
    home = {Q: (qb, 0), K: (kb, 0), V: (vb, 0), CK: (kb, 2 * span), CV: (vb, 2 * span)}

    def columns(which, head):
        return pl.ds(pl.multiple_of(which * 2 * HD + head * HD, HD), HD)

    def spread(part, head):
        buffer, first = home[part]
        landing = buffer.at[head, pl.ds(pl.multiple_of(first + seq * rows, rows), rows)]
        piece = seq // (8 // PIECES)
        for step in OTHERS:
            there = other(step)
            pltpu.make_async_remote_copy(
                src_ref=source[part].at[:, columns(head_slice(there[0], there[2], there[3]), head)],
                dst_ref=landing,
                send_sem=sends.at[part, head],
                recv_sem=arrivals.at[part, head, piece],
                device_id=device(*there),
                device_id_type=MESH,
            ).start()
        pltpu.make_async_copy(
            source[part].at[:, columns(mine, head)], landing, arrivals.at[part, head, piece]
        ).start()

    def shift():
        return pltpu.make_async_remote_copy(
            src_ref=resid,
            dst_ref=inc,
            send_sem=shifts.at[0],
            recv_sem=shifts.at[1],
            device_id=following,
            device_id_type=MESH,
        )

    is_last = section == 7

    @pl.when(is_last)
    def _():
        for part, head in ((K, 0), (V, 0), (K, 1), (V, 1), (Q, 0), (CK, 0), (CV, 0), (Q, 1), (CK, 1), (CV, 1)):
            spread(part, head)

    @pl.when(jnp.logical_not(is_last))
    def _():
        for head in range(2):
            for part in (K, V, Q, CK, CV):
                spread(part, head)

    @pl.when(jnp.logical_and(section < 7, section != 3))
    def _():
        shift().start()

    top[...] = jnp.full_like(top, LOW / 2)
    total[...] = jnp.zeros_like(total)
    acc[...] = jnp.zeros_like(acc)

    def settle(ref, sem):
        pltpu.make_async_copy(ref, ref, sem).wait()

    def arrived(part, head, piece):
        buffer, first = home[part]
        settle(buffer.at[head, pl.ds(first + piece * part_rows, part_rows)], arrivals.at[part, head, piece])

    def all_arrived(part, head):
        for piece in range(PIECES):
            arrived(part, head, piece)

    def stream(tree):
        return kb if tree == 0 else vb

    def fresh_arrived(tree, head, piece):
        block_ref = stream(tree).at[head, pl.ds(span + piece * part_rows, part_rows)]
        settle(block_ref, fresh.at[tree, head, piece])

    def pass_on(tree, head, piece, first, slot, target):
        return pltpu.make_async_remote_copy(
            src_ref=stream(tree).at[head, pl.ds(first + piece * part_rows, part_rows)],
            dst_ref=stream(tree).at[head, pl.ds(span + piece * part_rows, part_rows)],
            send_sem=relay_sends.at[tree, head, piece, slot],
            recv_sem=fresh.at[tree, head, piece],
            device_id=near[target],
            device_id_type=MESH,
        )

    def relay(tree, head, piece):
        for node, targets in TREES[tree].items():
            if node == 7:
                continue

            @pl.when(section == node)
            def _():
                fresh_arrived(tree, head, piece)
                for slot, target in enumerate(targets):
                    pass_on(tree, head, piece, span, slot, target).start()

    def leaf(tree):
        inner = [section != node for node in TREES[tree]]
        return functools.reduce(jnp.logical_and, inner)

    def take_fresh(tree, head, pieces):
        @pl.when(leaf(tree))
        def _():
            for piece in pieces:
                fresh_arrived(tree, head, piece)

    @pl.when(is_last)
    def _():
        for head in range(2):
            for tree, part in ((0, K), (1, V)):
                for piece in range(PIECES):
                    arrived(part, head, piece)
                    for slot, target in enumerate(TREES[tree][7]):
                        pass_on(tree, head, piece, 0, slot, target).start()
        all_arrived(Q, 0)

    @pl.when(jnp.logical_not(is_last))
    def _():
        for piece in range(PIECES):
            relay(0, 0, piece)
        all_arrived(K, 0)
        all_arrived(Q, 0)

    def do(action, *args):
        return functools.partial(action, *args)

    others = {
        (0, 0): [do(all_arrived, V, 0), do(relay, 1, 0, 0)],
        (0, 1): [do(relay, 1, 0, 1)],
        (1, 0): [do(relay, 1, 0, 2)],
        (1, 1): [do(relay, 1, 0, 3)] + [do(relay, 0, 1, p) for p in range(4)] + [do(all_arrived, CK, 0)],
        (2, 0): [do(all_arrived, CV, 0), do(relay, 1, 1, 0)],
        (2, 1): [do(relay, 1, 1, 1)],
        (3, 0): [do(relay, 1, 1, 2)],
        (3, 1): [do(relay, 1, 1, 3), do(take_fresh, 0, 0, (0, 1))],
        (4, 0): [do(take_fresh, 1, 0, (0, 1))],
        (4, 1): [do(take_fresh, 0, 0, (2, 3))],
        (5, 0): [do(take_fresh, 1, 0, (2, 3))],
        (5, 1): [do(all_arrived, Q, 1), do(all_arrived, K, 1)],
        (6, 0): [do(all_arrived, V, 1)],
        (7, 1): [do(take_fresh, 0, 1, (0, 1))],
        (8, 0): [do(take_fresh, 1, 1, (0, 1))],
        (8, 1): [do(take_fresh, 0, 1, (2, 3))],
        (9, 0): [do(take_fresh, 1, 1, (2, 3))],
        (9, 1): [do(all_arrived, CK, 1)],
        (10, 0): [do(all_arrived, CV, 1)],
    }
    last = {
        (3, 1): [do(all_arrived, CK, 0)],
        (4, 0): [do(all_arrived, CV, 0)],
        (5, 1): [do(all_arrived, Q, 1)],
        (9, 1): [do(all_arrived, CK, 1)],
        (10, 0): [do(all_arrived, CV, 1)],
    }

    def point(stage, at):
        for wanted, table in ((is_last, last), (jnp.logical_not(is_last), others)):
            for (number, where), actions in table.items():
                if where == at:

                    @pl.when(jnp.logical_and(stage == number, wanted))
                    def _():
                        for action in actions:
                            action()

    tiles = block // TILE

    def locate(stage):
        head, step = stage // 6, lax.rem(stage, 6)
        move = jnp.where(step < 2, 0, jnp.where(step < 4, 2, -2))
        index = step + jnp.where(jnp.logical_or(is_last, head == 1), 0, move)
        fresh_block = jnp.logical_and(index >= 2, index < 4)
        stored = index - jnp.where(jnp.logical_and(is_last, fresh_block), 2, 0)
        return head, index, pl.ds(pl.multiple_of(stored * block, block), block)

    def half_rows(half):
        return pl.ds(pl.multiple_of(half * block, block), block)

    def score(stage, half, out):
        head, _, keys = locate(stage)
        out[...] = lax.dot_general(
            kb[head, keys, :],
            qb[head, half_rows(half), :],
            (((1,), (1,)), ((), ())),
            preferred_element_type=F32,
        )

    def absorb(stage, half, scores):
        head, index, keys = locate(stage)
        biases = [
            jnp.concatenate(
                [jnp.full((1, TILE), bias[half * tiles + u, index * tiles + t], F32) for u in range(tiles)],
                axis=1,
            )
            for t in range(tiles)
        ]
        old = top[head, half]
        new = old
        for t in range(tiles):
            new = jnp.maximum(new, jnp.max(scores[pl.ds(t * TILE, TILE), :], axis=0, keepdims=True) + biases[t])
        top[head, half] = new
        factor = jnp.exp2((old - new) * RATE)
        expo = [
            jnp.exp2((scores[pl.ds(t * TILE, TILE), :] - (new - biases[t])) * RATE) for t in range(tiles)
        ]
        summed = total[head, half] * factor
        for part in expo:
            summed = summed + jnp.sum(part, axis=0, keepdims=True)
        total[head, half] = summed
        weight = jnp.concatenate([part.astype(BF16) for part in expo], axis=0)
        acc[head, half] = acc[head, half] * factor + lax.dot_general(
            vb[head, keys, :], weight, (((0,), (0,)), ((), ())), preferred_element_type=F32
        )

    def result(head):
        return attn.at[:, columns(mine, head)]

    def finish(head, half):
        ob[head, half_rows(half), :] = (acc[head, half] / total[head, half]).T.astype(BF16)
        for step in OTHERS:
            there = other(step)

            @pl.when(there[2] // 2 == half)
            def _():
                owner = there[2] * 2 + there[3]
                pltpu.make_async_remote_copy(
                    src_ref=ob.at[head, pl.ds(pl.multiple_of(owner * rows, rows), rows)],
                    dst_ref=result(head),
                    send_sem=out_sends.at[head],
                    recv_sem=out_arrivals.at[head],
                    device_id=device(*there),
                    device_id_type=MESH,
                ).start()

        @pl.when(x // 2 == half)
        def _():
            pltpu.make_async_copy(
                ob.at[head, pl.ds(pl.multiple_of(seq * rows, rows), rows)], result(head), out_arrivals.at[head]
            ).start()

    far = 1 - x // 2
    score(0, far, score_a)

    def stage_body(stage, carry):
        head, ends = stage // 6, lax.rem(stage, 6) == 5
        point(stage, 0)

        @pl.when(jnp.logical_and(stage == 6, section == 3))
        def _():
            shift().start()

        score(stage, 1 - far, score_b)
        absorb(stage, far, score_a)

        @pl.when(ends)
        def _():
            finish(head, far)

        point(stage, 1)
        score(jnp.minimum(stage + 1, 11), far, score_a)
        absorb(stage, 1 - far, score_b)

        @pl.when(ends)
        def _():
            finish(head, 1 - far)

        return carry

    lax.fori_loop(0, 12, stage_body, 0)

    for tree in range(2):
        for node, targets in TREES[tree].items():

            @pl.when(section == node)
            def _():
                for head in range(2):
                    for piece in range(PIECES):
                        for slot, target in enumerate(targets):
                            pass_on(tree, head, piece, span, slot, target).wait_send()

    @pl.when(section < 7)
    def _():
        shift().wait_send()

    @pl.when(section > 0)
    def _():
        shift().wait_recv()

    for head in range(2):
        for part in range(5):
            settle(home[part][0].at[head, pl.ds(0, 7 * rows)], sends.at[part, head])
        settle(ob.at[head, pl.ds(0, 7 * rows)], out_sends.at[head])
        settle(ob.at[head], out_arrivals.at[head])


def fused(q, k, v, ck, cv, resid, bias):
    rows, width = q.shape
    span = rows * 8
    half = span // 2
    dma = pltpu.SemaphoreType.DMA
    return pl.pallas_call(
        functools.partial(fused_kernel, span),
        out_shape=(jax.ShapeDtypeStruct((rows, width), BF16), jax.ShapeDtypeStruct((rows, width), BF16)),
        in_specs=[HBM] * 6 + [pl.BlockSpec(memory_space=pltpu.SMEM)],
        out_specs=[HBM] * 2,
        scratch_shapes=[
            pltpu.VMEM((2, span, HD), BF16),
            pltpu.VMEM((2, 3 * span, HD), BF16),
            pltpu.VMEM((2, 3 * span, HD), BF16),
            pltpu.VMEM((2, span, HD), BF16),
            pltpu.VMEM((half, half), F32),
            pltpu.VMEM((half, half), F32),
            pltpu.VMEM((2, 2, 1, half), F32),
            pltpu.VMEM((2, 2, 1, half), F32),
            pltpu.VMEM((2, 2, HD, half), F32),
            dma((5, 2)),
            dma((5, 2, PIECES)),
            dma((2,)),
            dma((2, 2, PIECES)),
            dma((2, 2, PIECES, 2)),
            dma((2,)),
            dma((2,)),
        ],
        name="fused",
        compiler_params=pltpu.CompilerParams(
            collective_id=0, has_side_effects=True, vmem_limit_bytes=60 * 2**20
        ),
    )(q, k, v, ck, cv, resid, bias)


def body(resid, span_q, span_k, span_v, cache_k, cache_v, cache_index, tile_mask):
    cached_k = lax.dynamic_index_in_dim(cache_k, cache_index[0], 0, keepdims=False)
    cached_v = lax.dynamic_index_in_dim(cache_v, cache_index[0], 0, keepdims=False)
    bias = jnp.where(tile_mask[0] > 0, 0.0, LOW).astype(F32)
    attn, incoming = fused(span_q[0], span_k[0], span_v[0], cached_k, cached_v, resid[0], bias)
    incoming = jnp.where(lax.axis_index("section") == 0, jnp.zeros_like(incoming), incoming)
    return (incoming.astype(F32) + attn.astype(F32)).astype(BF16)[None]


def solution(mesh):
    placed = (
        P("section", "seq", "mp"),
        P("section", "seq", "mp"),
        P("section", "seq", "mp"),
        P("section", "seq", "mp"),
        P(None, "seq", "mp"),
        P(None, "seq", "mp"),
        P("section"),
        P("section", None, None),
    )
    return jax.shard_map(
        body, mesh=mesh, in_specs=placed, out_specs=P("section", "seq", "mp"), check_vma=False
    )
```

```python
import functools
import math

import jax
import jax.numpy as jnp
from jax import lax
from jax.experimental import pallas as pl
from jax.experimental.pallas import tpu as pltpu
from jax.sharding import PartitionSpec as P

HD = 128
TILE = 128
MESH = pl.DeviceIdType.MESH
HBM = pl.BlockSpec(memory_space=pl.ANY)
VMEM = pl.BlockSpec(memory_space=pltpu.VMEM)
F32 = jnp.float32
BF16 = jnp.bfloat16
RATE = math.log2(math.e) / math.sqrt(HD)
OTHERS = ((2, 1), (1, 1), (3, 1), (2, 0), (0, 1), (1, 0), (3, 0))


def place():
    section, seq = lax.axis_index("section"), lax.axis_index("seq")
    return section // 4, lax.rem(section, 4), seq // 2, lax.rem(seq, 2)


def device(hi, y, x, lo):
    return {"section": hi * 4 + y, "seq": x * 2 + lo}


def head_slice(hi, x, lo):
    return 2 * x + lo + (1 - hi) * (1 - 2 * lo)


def other(step):
    hi, y, x, lo = place()
    return hi, y, lax.rem(x + step[0], 4), lax.rem(lo + step[1], 2)


TREES = (
    {7: ("up",), 4: ("up", "cross"), 5: ("up",), 0: ("up", "down"), 3: ("down",)},
    {7: ("down", "cross"), 6: ("down", "cross"), 3: ("up",), 5: ("down", "cross")},
)
PIECES = 4
NEARER = (4, 5, 0)
LOW = -1e30
Q, K, V, CK, CV = range(5)


def fused_kernel(
    span, q, k, v, cache_k, cache_v, resid, chosen, mask, out,
    qb, kb, vb, ob, score_a, score_b, top, total, acc, bias, all_ck, all_cv, ck, cv, attn, inc, via,
    sends, arrivals, shifts, fresh, relay_sends, out_sends, out_arrivals, loads, detours,
):
    hi, y, x, lo = place()
    section, seq = lax.axis_index("section"), lax.axis_index("seq")
    rows, block, part_rows = span // 8, span // 2, span // PIECES
    near = {
        "up": device(hi, lax.rem(y + 1, 4), x, lo),
        "down": device(hi, lax.rem(y + 3, 4), x, lo),
        "cross": device(1 - hi, y, x, 1 - lo),
    }
    following = {"section": lax.rem(section + 1, 8)}
    caches = [
        pltpu.make_async_copy(whole, held, loads.at[i])
        for i, (whole, held) in enumerate(((cache_k, all_ck), (cache_v, all_cv)))
    ]
    for copy in caches:
        copy.start()
    barrier = pltpu.get_barrier_semaphore()
    greeted = [device(*other(step)) for step in OTHERS] + list(near.values())
    greeted += [following, {"section": lax.rem(section + 7, 8)}]
    for target in greeted:
        pl.semaphore_signal(barrier, inc=1, device_id=target, device_id_type=MESH)

    @pl.when(section > 4)
    def _():
        pl.semaphore_signal(barrier, inc=1, device_id={"section": 3}, device_id_type=MESH)

    @pl.when(section == 4)
    def _():
        pl.semaphore_signal(barrier, inc=1, device_id={"section": 6}, device_id_type=MESH)

    extra = jnp.where(section == 3, 3, jnp.where(section == 6, 1, 0))
    pl.semaphore_wait(barrier, len(greeted) + extra)

    mine = head_slice(hi, x, lo)
    source = {Q: q, K: k, V: v, CK: ck, CV: cv}
    home = {Q: (qb, 0), K: (kb, 0), V: (vb, 0), CK: (kb, 2 * span), CV: (vb, 2 * span)}

    def columns(which, head):
        return pl.ds(pl.multiple_of(which * 2 * HD + head * HD, HD), HD)

    def spread(part, head, sub=None):
        buffer, first = home[part]
        if sub is None:
            taken, count, piece = 0, rows, seq // (8 // PIECES)
            place_there = first + seq * rows
        else:
            taken, count, piece = sub * TILE, TILE, sub
            place_there = first + sub * block + seq * TILE
        landing = buffer.at[head, pl.ds(pl.multiple_of(place_there, TILE), count)]
        for step in OTHERS:
            there = other(step)
            pltpu.make_async_remote_copy(
                src_ref=source[part].at[
                    pl.ds(taken, count), columns(head_slice(there[0], there[2], there[3]), head)
                ],
                dst_ref=landing,
                send_sem=sends.at[part, head],
                recv_sem=arrivals.at[part, head, piece],
                device_id=device(*there),
                device_id_type=MESH,
            ).start()
        pltpu.make_async_copy(
            source[part].at[pl.ds(taken, count), columns(mine, head)], landing, arrivals.at[part, head, piece]
        ).start()

    def shift():
        return pltpu.make_async_remote_copy(
            src_ref=resid,
            dst_ref=inc,
            send_sem=shifts.at[0],
            recv_sem=shifts.at[1],
            device_id=following,
            device_id_type=MESH,
        )

    quarter = rows // 4

    def detour(number):
        taken = resid.at[pl.ds(number * quarter, quarter)]
        return pltpu.make_async_remote_copy(
            src_ref=taken,
            dst_ref=inc.at[pl.ds(0, quarter)] if number == 0 else via,
            send_sem=shifts.at[0],
            recv_sem=shifts.at[1] if number == 0 else detours.at[0],
            device_id={"section": 4 + number},
            device_id_type=MESH,
        )

    def forward(number):
        return pltpu.make_async_remote_copy(
            src_ref=via,
            dst_ref=inc.at[pl.ds(number * quarter, quarter)],
            send_sem=detours.at[1],
            recv_sem=shifts.at[1],
            device_id={"section": 4},
            device_id_type=MESH,
        )

    def send_resid():
        @pl.when(jnp.logical_and(section < 7, section != 3))
        def _():
            shift().start()

    def send_detours():
        @pl.when(section == 3)
        def _():
            for number in range(4):
                detour(number).start()

    def forward_detours():
        for number in range(1, 4):

            @pl.when(section == 4 + number)
            def _():
                settle(via, detours.at[0])
                forward(number).start()

    is_last = section == 7

    @pl.when(is_last)
    def _():
        for part, head in ((K, 0), (V, 0), (K, 1), (V, 1), (Q, 0), (Q, 1)):
            spread(part, head)

    @pl.when(jnp.logical_not(is_last))
    def _():
        for head in range(2):
            for part in (K, V, Q):
                spread(part, head)

    def fill(tile, carry):
        lanes = [jnp.full((1, TILE), mask[u, tile], jnp.int32) for u in range(span // TILE)]
        bias[tile] = jnp.where(jnp.concatenate(lanes, axis=1) > 0, 0.0, LOW)
        return carry

    lax.fori_loop(0, 3 * span // TILE, fill, 0)
    for copy, held, picked in zip(caches, (all_ck, all_cv), (ck, cv)):
        copy.wait()
        for i in range(4):
            picked[pl.ds(i * quarter, quarter), :] = held[chosen[0], pl.ds(i * quarter, quarter), :]

    @pl.when(section == 0)
    def _():
        inc[...] = jnp.zeros_like(inc)

    top[...] = jnp.full_like(top, LOW / 2)
    total[...] = jnp.zeros_like(total)
    acc[...] = jnp.zeros_like(acc)

    def settle(ref, sem):
        pltpu.make_async_copy(ref, ref, sem).wait()

    def arrived(part, head, piece):
        buffer, first = home[part]
        settle(buffer.at[head, pl.ds(first + piece * part_rows, part_rows)], arrivals.at[part, head, piece])

    def cached_arrived(part, head, sub):
        buffer, first = home[part]
        settle(buffer.at[head, pl.ds(first + sub * block, block)], arrivals.at[part, head, sub])

    def all_arrived(part, head):
        for piece in range(PIECES):
            arrived(part, head, piece)

    def stream(tree):
        return kb if tree == 0 else vb

    def fresh_arrived(tree, head, piece):
        block_ref = stream(tree).at[head, pl.ds(span + piece * part_rows, part_rows)]
        settle(block_ref, fresh.at[tree, head, piece])

    def pass_on(tree, head, piece, first, slot, target):
        return pltpu.make_async_remote_copy(
            src_ref=stream(tree).at[head, pl.ds(first + piece * part_rows, part_rows)],
            dst_ref=stream(tree).at[head, pl.ds(span + piece * part_rows, part_rows)],
            send_sem=relay_sends.at[tree, head, piece, slot],
            recv_sem=fresh.at[tree, head, piece],
            device_id=near[target],
            device_id_type=MESH,
        )

    def relay(tree, head, piece, nodes=(0, 3, 4, 5, 6)):
        for node, targets in TREES[tree].items():
            if node not in nodes:
                continue

            @pl.when(section == node)
            def _():
                fresh_arrived(tree, head, piece)
                for slot, target in enumerate(targets):
                    pass_on(tree, head, piece, span, slot, target).start()

    def leaf(tree):
        inner = [section != node for node in TREES[tree]]
        return functools.reduce(jnp.logical_and, inner)

    def take_fresh(tree, head, pieces):
        @pl.when(leaf(tree))
        def _():
            for piece in pieces:
                fresh_arrived(tree, head, piece)

    @pl.when(is_last)
    def _():
        for head in range(2):
            for tree, part in ((0, K), (1, V)):
                for piece in range(PIECES):
                    arrived(part, head, piece)
                    for slot, target in enumerate(TREES[tree][7]):
                        pass_on(tree, head, piece, 0, slot, target).start()
        all_arrived(Q, 0)

    @pl.when(jnp.logical_not(is_last))
    def _():
        for piece in range(PIECES):
            relay(0, 0, piece, NEARER)
        all_arrived(K, 0)
        all_arrived(Q, 0)

    for head in range(2):
        for sub in range(2):
            for part in (CK, CV):
                spread(part, head, sub)

    def do(action, *args):
        return functools.partial(action, *args)

    late = {
        (5, 0): [send_resid],
        (7, 0): [send_detours],
        (7, 1): [do(cached_arrived, CK, 0, 0)],
        (8, 0): [do(cached_arrived, CV, 0, 0)],
        (8, 1): [do(cached_arrived, CK, 0, 1)],
        (9, 0): [do(cached_arrived, CV, 0, 1)],
        (9, 1): [do(cached_arrived, CK, 1, 0)],
        (10, 0): [do(cached_arrived, CV, 1, 0)],
        (10, 1): [do(cached_arrived, CK, 1, 1)],
        (11, 0): [do(cached_arrived, CV, 1, 1), forward_detours],
    }
    others = {
        (0, 0): [do(all_arrived, V, 0), do(relay, 1, 0, 0)],
        (0, 1): [do(relay, 1, 0, 1), do(relay, 0, 0, 0, (3,))],
        (1, 0): [do(relay, 1, 0, 2), do(relay, 0, 0, 1, (3,))],
        (1, 1): [do(relay, 1, 0, 3), do(relay, 0, 0, 2, (3,)), do(relay, 0, 0, 3, (3,))]
        + [do(relay, 0, 1, p, NEARER) for p in range(4)]
        + [do(take_fresh, 0, 0, (0, 1))],
        (2, 0): [do(take_fresh, 1, 0, (0, 1)), do(relay, 1, 1, 0), do(relay, 0, 1, 0, (3,))],
        (2, 1): [do(take_fresh, 0, 0, (2, 3)), do(relay, 1, 1, 1), do(relay, 0, 1, 1, (3,))],
        (3, 0): [do(take_fresh, 1, 0, (2, 3)), do(relay, 1, 1, 2), do(relay, 0, 1, 2, (3,))],
        (3, 1): [do(relay, 1, 1, 3), do(relay, 0, 1, 3, (3,)), do(all_arrived, Q, 1), do(all_arrived, K, 1)],
        (4, 0): [do(all_arrived, V, 1)],
        (5, 1): [do(take_fresh, 0, 1, (0, 1))],
        (6, 0): [do(take_fresh, 1, 1, (0, 1))],
        (6, 1): [do(take_fresh, 0, 1, (2, 3))],
        (7, 0): [do(take_fresh, 1, 1, (2, 3))],
    }
    last = {(3, 1): [do(all_arrived, Q, 1)]}

    def point(stage, at):
        for wanted, table in ((is_last, last), (jnp.logical_not(is_last), others), (section >= 0, late)):
            for (number, where), actions in table.items():
                if where == at:

                    @pl.when(jnp.logical_and(stage == number, wanted))
                    def _():
                        for action in actions:
                            action()

    tiles = block // TILE

    def locate(stage):
        pair = stage // 2
        cached = pair >= 4
        head = jnp.where(cached, pair - 4, pair // 2)
        kind = jnp.where(cached, 2, lax.rem(pair, 2))
        index = 2 * kind + lax.rem(stage, 2)
        stored = index - jnp.where(jnp.logical_and(is_last, kind == 1), 2, 0)
        first = jnp.where(cached, 4 * tiles + lax.rem(stage, 2), index * tiles)
        return head, (first, jnp.where(cached, 2, 1)), pl.ds(pl.multiple_of(stored * block, block), block)

    def half_rows(half):
        return pl.ds(pl.multiple_of(half * block, block), block)

    def score(stage, half, out):
        head, _, keys = locate(stage)
        out[...] = lax.dot_general(
            kb[head, keys, :],
            qb[head, half_rows(half), :],
            (((1,), (1,)), ((), ())),
            preferred_element_type=F32,
        )

    def absorb(stage, half, scores):
        head, (first, pace), keys = locate(stage)
        biases = [bias[first + t * pace, :, half_rows(half)] for t in range(tiles)]
        old = top[head, half]
        new = old
        for t in range(tiles):
            new = jnp.maximum(new, jnp.max(scores[pl.ds(t * TILE, TILE), :], axis=0, keepdims=True) + biases[t])
        top[head, half] = new
        factor = jnp.exp2((old - new) * RATE)
        expo = [
            jnp.exp2((scores[pl.ds(t * TILE, TILE), :] - (new - biases[t])) * RATE) for t in range(tiles)
        ]
        summed = total[head, half] * factor
        for part in expo:
            summed = summed + jnp.sum(part, axis=0, keepdims=True)
        total[head, half] = summed
        weight = jnp.concatenate([part.astype(BF16) for part in expo], axis=0)
        acc[head, half] = acc[head, half] * factor + lax.dot_general(
            vb[head, keys, :], weight, (((0,), (0,)), ((), ())), preferred_element_type=F32
        )

    def result(head):
        return attn.at[:, columns(mine, head)]

    def finish(head, half):
        ob[head, half_rows(half), :] = (acc[head, half] / total[head, half]).T.astype(BF16)
        for step in OTHERS:
            there = other(step)

            @pl.when(there[2] // 2 == half)
            def _():
                owner = there[2] * 2 + there[3]
                pltpu.make_async_remote_copy(
                    src_ref=ob.at[head, pl.ds(pl.multiple_of(owner * rows, rows), rows)],
                    dst_ref=result(head),
                    send_sem=out_sends.at[head],
                    recv_sem=out_arrivals.at[head],
                    device_id=device(*there),
                    device_id_type=MESH,
                ).start()

        @pl.when(x // 2 == half)
        def _():
            pltpu.make_async_copy(
                ob.at[head, pl.ds(pl.multiple_of(seq * rows, rows), rows)], result(head), out_arrivals.at[head]
            ).start()

    far = 1 - x // 2
    score(0, far, score_a)

    def stage_body(stage, carry):
        head, ends = stage // 11, jnp.logical_or(stage == 9, stage == 11)
        point(stage, 0)
        score(stage, 1 - far, score_b)
        absorb(stage, far, score_a)

        @pl.when(ends)
        def _():
            finish(head, far)

        point(stage, 1)
        score(jnp.minimum(stage + 1, 11), far, score_a)
        absorb(stage, 1 - far, score_b)

        @pl.when(ends)
        def _():
            finish(head, 1 - far)

        return carry

    lax.fori_loop(0, 12, stage_body, 0)

    for tree in range(2):
        for node, targets in TREES[tree].items():

            @pl.when(section == node)
            def _():
                for head in range(2):
                    for piece in range(PIECES):
                        for slot, target in enumerate(targets):
                            pass_on(tree, head, piece, span, slot, target).wait_send()

    @pl.when(section < 7)
    def _():
        settle(resid, shifts.at[0])

    @pl.when(section > 4)
    def _():
        settle(via, detours.at[1])

    @pl.when(section > 0)
    def _():
        settle(inc, shifts.at[1])

    for head in range(2):
        for part in range(5):
            settle(home[part][0].at[head, pl.ds(0, 7 * rows)], sends.at[part, head])
        settle(ob.at[head, pl.ds(0, 7 * rows)], out_sends.at[head])
        settle(ob.at[head], out_arrivals.at[head])
    out[...] = (inc[...].astype(F32) + attn[...].astype(F32)).astype(BF16)


def fused(q, k, v, cache_k, cache_v, resid, chosen, mask):
    rows, width = q.shape
    span = rows * 8
    half = span // 2
    dma = pltpu.SemaphoreType.DMA
    smem = pl.BlockSpec(memory_space=pltpu.SMEM)
    return pl.pallas_call(
        functools.partial(fused_kernel, span),
        out_shape=jax.ShapeDtypeStruct((rows, width), BF16),
        in_specs=[HBM] * 6 + [smem] * 2,
        out_specs=VMEM,
        scratch_shapes=[
            pltpu.VMEM((2, span, HD), BF16),
            pltpu.VMEM((2, 3 * span, HD), BF16),
            pltpu.VMEM((2, 3 * span, HD), BF16),
            pltpu.VMEM((2, span, HD), BF16),
            pltpu.VMEM((half, half), F32),
            pltpu.VMEM((half, half), F32),
            pltpu.VMEM((2, 2, 1, half), F32),
            pltpu.VMEM((2, 2, 1, half), F32),
            pltpu.VMEM((2, 2, HD, half), F32),
            pltpu.VMEM((3 * span // TILE, 1, span), F32),
            pltpu.VMEM(cache_k.shape, BF16),
            pltpu.VMEM(cache_v.shape, BF16),
            pltpu.VMEM((rows, width), BF16),
            pltpu.VMEM((rows, width), BF16),
            pltpu.VMEM((rows, width), BF16),
            pltpu.VMEM((rows, width), BF16),
            pltpu.VMEM((rows // 4, width), BF16),
            dma((5, 2)),
            dma((5, 2, PIECES)),
            dma((2,)),
            dma((2, 2, PIECES)),
            dma((2, 2, PIECES, 2)),
            dma((2,)),
            dma((2,)),
            dma((2,)),
            dma((2,)),
        ],
        name="fused",
        compiler_params=pltpu.CompilerParams(
            collective_id=0, has_side_effects=True, vmem_limit_bytes=60 * 2**20
        ),
    )(q, k, v, cache_k, cache_v, resid, chosen, mask)


def body(resid, span_q, span_k, span_v, cache_k, cache_v, cache_index, tile_mask):
    return fused(
        span_q[0], span_k[0], span_v[0], cache_k, cache_v, resid[0], cache_index, tile_mask[0]
    )[None]


def solution(mesh):
    placed = (
        P("section", "seq", "mp"),
        P("section", "seq", "mp"),
        P("section", "seq", "mp"),
        P("section", "seq", "mp"),
        P(None, "seq", "mp"),
        P(None, "seq", "mp"),
        P("section"),
        P("section", None, None),
    )
    return jax.shard_map(
        body, mesh=mesh, in_specs=placed, out_specs=P("section", "seq", "mp"), check_vma=False
    )
```

```python
import functools
import math

import jax
import jax.numpy as jnp
from jax import lax
from jax.experimental import pallas as pl
from jax.experimental.pallas import tpu as pltpu
from jax.sharding import PartitionSpec as P

HD = 128
TILE = 128
MESH = pl.DeviceIdType.MESH
HBM = pl.BlockSpec(memory_space=pl.ANY)
VMEM = pl.BlockSpec(memory_space=pltpu.VMEM)
F32 = jnp.float32
BF16 = jnp.bfloat16
RATE = math.log2(math.e) / math.sqrt(HD)
OTHERS = ((2, 1), (1, 1), (3, 1), (2, 0), (0, 1), (1, 0), (3, 0))


def place():
    section, seq = lax.axis_index("section"), lax.axis_index("seq")
    return section // 4, lax.rem(section, 4), seq // 2, lax.rem(seq, 2)


def device(hi, y, x, lo):
    return {"section": hi * 4 + y, "seq": x * 2 + lo}


def head_slice(hi, x, lo):
    return 2 * x + lo + (1 - hi) * (1 - 2 * lo)


def other(step):
    hi, y, x, lo = place()
    return hi, y, lax.rem(x + step[0], 4), lax.rem(lo + step[1], 2)


TREES = (
    {7: ("up",), 4: ("up", "cross"), 5: ("up",), 0: ("up", "down"), 3: ("down",)},
    {7: ("down", "cross"), 6: ("down", "cross"), 3: ("up",), 5: ("down", "cross")},
)
PIECES = 4
EARLY = 3
LOW = -1e30
Q, K, V, CK, CV = range(5)


def fused_kernel(
    span, q, k, v, cache_k, cache_v, resid, chosen, mask, out,
    qb, kb, vb, ob, score_a, score_b, top, total, acc, bias, all_ck, all_cv, ck, cv, attn, inc, via,
    sends, arrivals, shifts, fresh, relay_sends, out_sends, out_arrivals, loads, detours,
):
    hi, y, x, lo = place()
    section, seq = lax.axis_index("section"), lax.axis_index("seq")
    rows, block, part_rows = span // 8, span // 2, span // PIECES
    near = {
        "up": device(hi, lax.rem(y + 1, 4), x, lo),
        "down": device(hi, lax.rem(y + 3, 4), x, lo),
        "cross": device(1 - hi, y, x, 1 - lo),
    }
    following = {"section": lax.rem(section + 1, 8)}
    caches = [
        pltpu.make_async_copy(whole, held, loads.at[i])
        for i, (whole, held) in enumerate(((cache_k, all_ck), (cache_v, all_cv)))
    ]
    for copy in caches:
        copy.start()
    barrier = pltpu.get_barrier_semaphore()
    greeted = [device(*other(step)) for step in OTHERS] + list(near.values())
    greeted += [following, {"section": lax.rem(section + 7, 8)}]
    for target in greeted:
        pl.semaphore_signal(barrier, inc=1, device_id=target, device_id_type=MESH)

    @pl.when(section > 4)
    def _():
        pl.semaphore_signal(barrier, inc=1, device_id={"section": 3}, device_id_type=MESH)

    @pl.when(section == 4)
    def _():
        pl.semaphore_signal(barrier, inc=1, device_id={"section": 6}, device_id_type=MESH)

    extra = jnp.where(section == 3, 3, jnp.where(section == 6, 1, 0))
    pl.semaphore_wait(barrier, len(greeted) + extra)

    mine = head_slice(hi, x, lo)
    source = {Q: q, K: k, V: v, CK: ck, CV: cv}
    home = {Q: (qb, 0), K: (kb, 0), V: (vb, 0), CK: (kb, 2 * span), CV: (vb, 2 * span)}

    def columns(which, head):
        return pl.ds(pl.multiple_of(which * 2 * HD + head * HD, HD), HD)

    def spread(part, head, sub=None):
        buffer, first = home[part]
        if sub is None:
            taken, count, piece = 0, rows, seq // (8 // PIECES)
            place_there = first + seq * rows
        else:
            taken, count, piece = sub * TILE, TILE, sub
            place_there = first + sub * block + seq * TILE
        landing = buffer.at[head, pl.ds(pl.multiple_of(place_there, TILE), count)]
        for step in OTHERS:
            there = other(step)
            pltpu.make_async_remote_copy(
                src_ref=source[part].at[
                    pl.ds(taken, count), columns(head_slice(there[0], there[2], there[3]), head)
                ],
                dst_ref=landing,
                send_sem=sends.at[part, head],
                recv_sem=arrivals.at[part, head, piece],
                device_id=device(*there),
                device_id_type=MESH,
            ).start()
        pltpu.make_async_copy(
            source[part].at[pl.ds(taken, count), columns(mine, head)], landing, arrivals.at[part, head, piece]
        ).start()

    def shift(number):
        strip = pl.ds(number * (rows // 8), rows // 8)
        return pltpu.make_async_remote_copy(
            src_ref=resid.at[strip],
            dst_ref=inc.at[strip],
            send_sem=shifts.at[0],
            recv_sem=shifts.at[1],
            device_id=following,
            device_id_type=MESH,
        )

    quarter = rows // 4

    def detour(number):
        taken = resid.at[pl.ds(number * quarter, quarter)]
        return pltpu.make_async_remote_copy(
            src_ref=taken,
            dst_ref=inc.at[pl.ds(0, quarter)] if number == 0 else via,
            send_sem=shifts.at[0],
            recv_sem=shifts.at[1] if number == 0 else detours.at[0],
            device_id={"section": 4 + number},
            device_id_type=MESH,
        )

    def forward(number):
        return pltpu.make_async_remote_copy(
            src_ref=via,
            dst_ref=inc.at[pl.ds(number * quarter, quarter)],
            send_sem=detours.at[1],
            recv_sem=shifts.at[1],
            device_id={"section": 4},
            device_id_type=MESH,
        )

    shared = functools.reduce(jnp.logical_or, [section == node for node in (0, 4, 5)])

    def send_resid(numbers, where):
        @pl.when(jnp.logical_and(where, jnp.logical_and(section < 7, section != 3)))
        def _():
            for number in numbers:
                shift(number).start()

    def send_detour(number):
        @pl.when(section == 3)
        def _():
            detour(number).start()

    def forward_detours():
        for number in range(1, 4):

            @pl.when(section == 4 + number)
            def _():
                settle(via, detours.at[0])
                forward(number).start()

    is_last = section == 7

    send_resid(range(EARLY), section >= 0)

    @pl.when(is_last)
    def _():
        for part, head in ((K, 0), (V, 0), (K, 1)):
            spread(part, head)

    @pl.when(jnp.logical_not(is_last))
    def _():
        for part in (K, V, Q):
            spread(part, 0)

    send_resid(range(EARLY, 8), jnp.logical_not(shared))

    def fill(tile, carry):
        lanes = [jnp.full((1, TILE), mask[u, tile], jnp.int32) for u in range(span // TILE)]
        allowed = jnp.concatenate(lanes, axis=1)
        bias[tile] = jnp.where(allowed > 0, 0.0, LOW)

        @pl.when(jnp.logical_and(is_last, tile < span // TILE))
        def _():
            again = [jnp.full((1, TILE), mask[u, tile + span // TILE], jnp.int32) for u in range(span // TILE)]
            times = allowed + jnp.concatenate(again, axis=1)
            bias[tile] = jnp.where(times > 1, 1.0 / RATE, jnp.where(times > 0, 0.0, LOW))

        return carry

    lax.fori_loop(0, 3 * span // TILE, fill, 0)
    for copy, held, picked in zip(caches, (all_ck, all_cv), (ck, cv)):
        copy.wait()
        for i in range(4):
            picked[pl.ds(i * quarter, quarter), :] = held[chosen[0], pl.ds(i * quarter, quarter), :]

    def spread_cached(part, head):
        for sub in range(2):
            spread(part, head, sub)

    @pl.when(section == 0)
    def _():
        inc[...] = jnp.zeros_like(inc)

    top[...] = jnp.full_like(top, LOW / 2)
    total[...] = jnp.zeros_like(total)
    acc[...] = jnp.zeros_like(acc)

    def settle(ref, sem):
        pltpu.make_async_copy(ref, ref, sem).wait()

    def arrived(part, head, piece):
        buffer, first = home[part]
        settle(buffer.at[head, pl.ds(first + piece * part_rows, part_rows)], arrivals.at[part, head, piece])

    def cached_arrived(part, head, sub):
        buffer, first = home[part]
        settle(buffer.at[head, pl.ds(first + sub * block, block)], arrivals.at[part, head, sub])

    def all_arrived(part, head):
        for piece in range(PIECES):
            arrived(part, head, piece)

    def stream(tree):
        return kb if tree == 0 else vb

    def fresh_arrived(tree, head, piece):
        block_ref = stream(tree).at[head, pl.ds(span + piece * part_rows, part_rows)]
        settle(block_ref, fresh.at[tree, head, piece])

    def pass_on(tree, head, piece, first, slot, target):
        return pltpu.make_async_remote_copy(
            src_ref=stream(tree).at[head, pl.ds(first + piece * part_rows, part_rows)],
            dst_ref=stream(tree).at[head, pl.ds(span + piece * part_rows, part_rows)],
            send_sem=relay_sends.at[tree, head, piece, slot],
            recv_sem=fresh.at[tree, head, piece],
            device_id=near[target],
            device_id_type=MESH,
        )

    def relay(tree, head, piece, nodes=(0, 3, 4, 5, 6)):
        for node, targets in TREES[tree].items():
            if node not in nodes:
                continue

            @pl.when(section == node)
            def _():
                fresh_arrived(tree, head, piece)
                for slot, target in enumerate(targets):
                    pass_on(tree, head, piece, span, slot, target).start()

    def leaf(tree):
        inner = [section != node for node in TREES[tree]]
        return functools.reduce(jnp.logical_and, inner)

    def take_fresh(tree, head, pieces):
        @pl.when(leaf(tree))
        def _():
            for piece in pieces:
                fresh_arrived(tree, head, piece)

    def do(action, *args):
        return functools.partial(action, *args)

    @pl.when(is_last)
    def _():
        following_sends = iter((do(spread, V, 1), do(spread, Q, 0), do(spread, Q, 1), do(spread_cached, CK, 0)))
        for head in range(2):
            for tree, part in ((0, K), (1, V)):
                for piece in range(PIECES):
                    arrived(part, head, piece)
                    for slot, target in enumerate(TREES[tree][7]):
                        pass_on(tree, head, piece, 0, slot, target).start()
                next(following_sends)()
        all_arrived(Q, 0)
        spread_cached(CV, 0)

    @pl.when(jnp.logical_not(is_last))
    def _():
        all_arrived(K, 0)
        spread_cached(CK, 0)
        for piece in range(2):
            relay(0, 0, piece, (4,))
        all_arrived(V, 0)
        spread_cached(CV, 0)
        for piece in range(2, 4):
            relay(0, 0, piece, (4,))
        all_arrived(Q, 0)
        spread(Q, 1)

    def tail(first):
        return {
            (first - 1, 1): [do(cached_arrived, CK, 1, 0)],
            (first, 0): [do(cached_arrived, CV, 1, 0)],
            (first, 1): [do(cached_arrived, CK, 1, 1)],
            (first + 1, 0): [do(cached_arrived, CV, 1, 1), forward_detours],
        }

    others = {
        (0, 0): [do(relay, 1, 0, 0), do(relay, 0, 0, 0, (0, 5))],
        (0, 1): [do(relay, 1, 0, 1), do(relay, 0, 0, 1, (0, 5))],
        (1, 0): [do(relay, 1, 0, 2), do(relay, 0, 0, 2, (0, 5)), do(relay, 0, 0, 0, (3,))],
        (1, 1): [do(relay, 1, 0, 3), do(relay, 0, 0, 3, (0, 5))]
        + [do(relay, 0, 0, p, (3,)) for p in (1, 2, 3)]
        + [do(relay, 0, 1, p, (4,)) for p in range(4)]
        + [do(cached_arrived, CK, 0, 0), do(spread, K, 1)],
        (2, 0): [do(cached_arrived, CV, 0, 0), do(relay, 1, 1, 0, (6, 3)), do(relay, 0, 1, 0, (0, 5))],
        (2, 1): [
            do(spread, V, 1),
            do(cached_arrived, CK, 0, 1),
            do(relay, 1, 1, 1, (6, 3)),
            do(relay, 0, 1, 1, (0, 5)),
        ],
        (3, 0): [
            do(cached_arrived, CV, 0, 1),
            do(relay, 1, 1, 2, (6, 3)),
            do(relay, 0, 1, 2, (0, 5)),
            do(relay, 1, 1, 0, (5,)),
            do(relay, 0, 1, 0, (3,)),
        ],
        (3, 1): [
            do(spread_cached, CK, 1),
            do(send_resid, (3, 4), shared),
            do(relay, 1, 1, 3, (6, 3)),
            do(relay, 0, 1, 3, (0, 5)),
            do(relay, 1, 1, 1, (5,)),
            do(relay, 0, 1, 1, (3,)),
            do(take_fresh, 0, 0, (0, 1)),
        ],
        (4, 0): [
            do(send_resid, (5,), shared),
            do(take_fresh, 1, 0, (0, 1)),
            do(relay, 1, 1, 2, (5,)),
            do(relay, 0, 1, 2, (3,)),
        ],
        (4, 1): [
            do(take_fresh, 0, 0, (2, 3)),
            do(relay, 1, 1, 3, (5,)),
            do(relay, 0, 1, 3, (3,)),
            do(spread_cached, CV, 1),
            do(send_resid, (6, 7), shared),
        ],
        (5, 0): [do(take_fresh, 1, 0, (2, 3))],
        (5, 1): [do(all_arrived, Q, 1), do(take_fresh, 0, 1, (0, 1))],
        (6, 0): [do(send_detour, 1), do(take_fresh, 1, 1, (0, 1))],
        (6, 1): [do(take_fresh, 0, 1, (2, 3))],
        (7, 0): [do(send_detour, 2), do(take_fresh, 1, 1, (2, 3))],
        (7, 1): [do(all_arrived, K, 1)],
        (8, 0): [do(send_detour, 3), do(all_arrived, V, 1)],
        (9, 0): [do(send_detour, 0)],
        **tail(10),
    }
    last = {
        (1, 1): [do(all_arrived, Q, 1), do(spread_cached, CK, 1)],
        (2, 1): [do(spread_cached, CV, 1)],
        (3, 1): [do(cached_arrived, CK, 0, 0)],
        (4, 0): [do(cached_arrived, CV, 0, 0)],
        (4, 1): [do(cached_arrived, CK, 0, 1)],
        (5, 0): [do(cached_arrived, CV, 0, 1)],
        **tail(6),
    }

    def point(stage, at):
        for wanted, table in ((is_last, last), (jnp.logical_not(is_last), others)):
            for (number, where), actions in table.items():
                if where == at:

                    @pl.when(jnp.logical_and(stage == number, wanted))
                    def _():
                        for action in actions:
                            action()

    tiles = block // TILE

    def locate(stage):
        pair = stage // 2
        head = jnp.where(is_last, lax.rem(pair, 2), pair // 3)
        kind_others = jnp.where(pair < 3, lax.rem(2 * pair, 3), lax.rem(2 * pair + 1, 3))
        kind = jnp.where(is_last, 2 * (pair // 2), kind_others)
        cached = kind == 2
        index = 2 * kind + lax.rem(stage, 2)
        first = jnp.where(cached, 4 * tiles + lax.rem(stage, 2), index * tiles)
        return head, (first, jnp.where(cached, 2, 1)), pl.ds(pl.multiple_of(index * block, block), block)

    def half_rows(half):
        return pl.ds(pl.multiple_of(half * block, block), block)

    def score(stage, half, out):
        head, _, keys = locate(stage)
        out[...] = lax.dot_general(
            kb[head, keys, :],
            qb[head, half_rows(half), :],
            (((1,), (1,)), ((), ())),
            preferred_element_type=F32,
        )

    def absorb(stage, half, scores):
        head, (first, pace), keys = locate(stage)
        biases = [bias[first + t * pace, :, half_rows(half)] for t in range(tiles)]
        old = top[head, half]
        new = old
        for t in range(tiles):
            new = jnp.maximum(new, jnp.max(scores[pl.ds(t * TILE, TILE), :], axis=0, keepdims=True) + biases[t])
        top[head, half] = new
        factor = jnp.exp2((old - new) * RATE)
        expo = [
            jnp.exp2((scores[pl.ds(t * TILE, TILE), :] - (new - biases[t])) * RATE) for t in range(tiles)
        ]
        summed = total[head, half] * factor
        for part in expo:
            summed = summed + jnp.sum(part, axis=0, keepdims=True)
        total[head, half] = summed
        weight = jnp.concatenate([part.astype(BF16) for part in expo], axis=0)
        acc[head, half] = acc[head, half] * factor + lax.dot_general(
            vb[head, keys, :], weight, (((0,), (0,)), ((), ())), preferred_element_type=F32
        )

    def result(head):
        return attn.at[:, columns(mine, head)]

    def finish(head, half):
        ob[head, half_rows(half), :] = (acc[head, half] / total[head, half]).T.astype(BF16)
        for step in OTHERS:
            there = other(step)

            @pl.when(there[2] // 2 == half)
            def _():
                owner = there[2] * 2 + there[3]
                pltpu.make_async_remote_copy(
                    src_ref=ob.at[head, pl.ds(pl.multiple_of(owner * rows, rows), rows)],
                    dst_ref=result(head),
                    send_sem=out_sends.at[head],
                    recv_sem=out_arrivals.at[head],
                    device_id=device(*there),
                    device_id_type=MESH,
                ).start()

        @pl.when(x // 2 == half)
        def _():
            pltpu.make_async_copy(
                ob.at[head, pl.ds(pl.multiple_of(seq * rows, rows), rows)], result(head), out_arrivals.at[head]
            ).start()

    far = 1 - x // 2
    stages = jnp.where(is_last, 8, 12)
    score(0, far, score_a)

    def stage_body(stage, carry):
        head = stage // (stages - 1)
        ends = jnp.logical_or(stage == 5, stage == stages - 1)
        point(stage, 0)
        score(stage, 1 - far, score_b)
        absorb(stage, far, score_a)

        @pl.when(ends)
        def _():
            finish(head, far)

        point(stage, 1)
        score(jnp.minimum(stage + 1, stages - 1), far, score_a)
        absorb(stage, 1 - far, score_b)

        @pl.when(ends)
        def _():
            finish(head, 1 - far)

        return carry

    lax.fori_loop(0, stages, stage_body, 0)

    for tree in range(2):
        for node, targets in TREES[tree].items():

            @pl.when(section == node)
            def _():
                for head in range(2):
                    for piece in range(PIECES):
                        for slot, target in enumerate(targets):
                            pass_on(tree, head, piece, span, slot, target).wait_send()

    @pl.when(section < 7)
    def _():
        settle(resid, shifts.at[0])

    @pl.when(section > 4)
    def _():
        settle(via, detours.at[1])

    @pl.when(section > 0)
    def _():
        settle(inc, shifts.at[1])

    for head in range(2):
        for part in range(5):
            settle(home[part][0].at[head, pl.ds(0, 7 * rows)], sends.at[part, head])
        settle(ob.at[head, pl.ds(0, 7 * rows)], out_sends.at[head])
        settle(ob.at[head], out_arrivals.at[head])
    out[...] = (inc[...].astype(F32) + attn[...].astype(F32)).astype(BF16)


def fused(q, k, v, cache_k, cache_v, resid, chosen, mask):
    rows, width = q.shape
    span = rows * 8
    half = span // 2
    dma = pltpu.SemaphoreType.DMA
    smem = pl.BlockSpec(memory_space=pltpu.SMEM)
    return pl.pallas_call(
        functools.partial(fused_kernel, span),
        out_shape=jax.ShapeDtypeStruct((rows, width), BF16),
        in_specs=[HBM] * 6 + [smem] * 2,
        out_specs=VMEM,
        scratch_shapes=[
            pltpu.VMEM((2, span, HD), BF16),
            pltpu.VMEM((2, 3 * span, HD), BF16),
            pltpu.VMEM((2, 3 * span, HD), BF16),
            pltpu.VMEM((2, span, HD), BF16),
            pltpu.VMEM((half, half), F32),
            pltpu.VMEM((half, half), F32),
            pltpu.VMEM((2, 2, 1, half), F32),
            pltpu.VMEM((2, 2, 1, half), F32),
            pltpu.VMEM((2, 2, HD, half), F32),
            pltpu.VMEM((3 * span // TILE, 1, span), F32),
            pltpu.VMEM(cache_k.shape, BF16),
            pltpu.VMEM(cache_v.shape, BF16),
            pltpu.VMEM((rows, width), BF16),
            pltpu.VMEM((rows, width), BF16),
            pltpu.VMEM((rows, width), BF16),
            pltpu.VMEM((rows, width), BF16),
            pltpu.VMEM((rows // 4, width), BF16),
            dma((5, 2)),
            dma((5, 2, PIECES)),
            dma((2,)),
            dma((2, 2, PIECES)),
            dma((2, 2, PIECES, 2)),
            dma((2,)),
            dma((2,)),
            dma((2,)),
            dma((2,)),
        ],
        name="fused",
        compiler_params=pltpu.CompilerParams(
            collective_id=0, has_side_effects=True, vmem_limit_bytes=60 * 2**20
        ),
    )(q, k, v, cache_k, cache_v, resid, chosen, mask)


def body(resid, span_q, span_k, span_v, cache_k, cache_v, cache_index, tile_mask):
    return fused(
        span_q[0], span_k[0], span_v[0], cache_k, cache_v, resid[0], cache_index, tile_mask[0]
    )[None]


def solution(mesh):
    placed = (
        P("section", "seq", "mp"),
        P("section", "seq", "mp"),
        P("section", "seq", "mp"),
        P("section", "seq", "mp"),
        P(None, "seq", "mp"),
        P(None, "seq", "mp"),
        P("section"),
        P("section", None, None),
    )
    return jax.shard_map(
        body, mesh=mesh, in_specs=placed, out_specs=P("section", "seq", "mp"), check_vma=False
    )
```

```python
import functools
import math

import jax
import jax.numpy as jnp
from jax import lax
from jax.experimental import pallas as pl
from jax.experimental.pallas import tpu as pltpu
from jax.sharding import PartitionSpec as P

HD = 128
TILE = 128
MESH = pl.DeviceIdType.MESH
HBM = pl.BlockSpec(memory_space=pl.ANY)
VMEM = pl.BlockSpec(memory_space=pltpu.VMEM)
F32 = jnp.float32
BF16 = jnp.bfloat16
RATE = math.log2(math.e) / math.sqrt(HD)
OTHERS = ((2, 1), (1, 1), (3, 1), (2, 0), (0, 1), (1, 0), (3, 0))


def place():
    section, seq = lax.axis_index("section"), lax.axis_index("seq")
    return section // 4, lax.rem(section, 4), seq // 2, lax.rem(seq, 2)


def device(hi, y, x, lo):
    return {"section": hi * 4 + y, "seq": x * 2 + lo}


def head_slice(hi, x, lo):
    return 2 * x + lo + (1 - hi) * (1 - 2 * lo)


def other(step):
    hi, y, x, lo = place()
    return hi, y, lax.rem(x + step[0], 4), lax.rem(lo + step[1], 2)


TREES = (
    {7: ("up",), 4: ("up", "cross"), 5: ("up",), 0: ("up", "down"), 3: ("down",)},
    {7: ("down", "cross"), 6: ("down", "cross"), 3: ("up",), 5: ("down", "cross")},
)
PIECES = 4
EARLY = 3
LOW = -1e30
Q, K, V, CK, CV = range(5)


def fused_kernel(
    span, q, k, v, cache_k, cache_v, resid, chosen, mask, out,
    qb, kb, vb, ob, score_a, score_b, top, total, acc, bias, all_ck, all_cv, ck, cv, attn, inc, via,
    sends, arrivals, shifts, fresh, relay_sends, out_sends, out_arrivals, loads, detours,
):
    hi, y, x, lo = place()
    section, seq = lax.axis_index("section"), lax.axis_index("seq")
    rows, block, part_rows = span // 8, span // 2, span // PIECES
    near = {
        "up": device(hi, lax.rem(y + 1, 4), x, lo),
        "down": device(hi, lax.rem(y + 3, 4), x, lo),
        "cross": device(1 - hi, y, x, 1 - lo),
    }
    following = {"section": lax.rem(section + 1, 8)}
    caches = [
        pltpu.make_async_copy(whole, held, loads.at[i])
        for i, (whole, held) in enumerate(((cache_k, all_ck), (cache_v, all_cv)))
    ]
    for copy in caches:
        copy.start()
    barrier = pltpu.get_barrier_semaphore()
    greeted = [device(*other(step)) for step in OTHERS] + list(near.values())
    greeted += [following, {"section": lax.rem(section + 7, 8)}]
    for target in greeted:
        pl.semaphore_signal(barrier, inc=1, device_id=target, device_id_type=MESH)

    @pl.when(section > 4)
    def _():
        pl.semaphore_signal(barrier, inc=1, device_id={"section": 3}, device_id_type=MESH)

    @pl.when(section == 4)
    def _():
        pl.semaphore_signal(barrier, inc=1, device_id={"section": 6}, device_id_type=MESH)

    extra = jnp.where(section == 3, 3, jnp.where(section == 6, 1, 0))
    pl.semaphore_wait(barrier, len(greeted) + extra)

    mine = head_slice(hi, x, lo)
    source = {Q: q, K: k, V: v, CK: ck, CV: cv}
    home = {Q: (qb, 0), K: (kb, 0), V: (vb, 0), CK: (kb, 2 * span), CV: (vb, 2 * span)}

    def columns(which, head):
        return pl.ds(pl.multiple_of(which * 2 * HD + head * HD, HD), HD)

    def spread(part, head, sub=None):
        buffer, first = home[part]
        if sub is None:
            taken, count, piece = 0, rows, seq // (8 // PIECES)
            place_there = first + seq * rows
        else:
            taken, count, piece = sub * TILE, TILE, sub
            place_there = first + sub * block + seq * TILE
        landing = buffer.at[head, pl.ds(pl.multiple_of(place_there, TILE), count)]
        for step in OTHERS:
            there = other(step)
            pltpu.make_async_remote_copy(
                src_ref=source[part].at[
                    pl.ds(taken, count), columns(head_slice(there[0], there[2], there[3]), head)
                ],
                dst_ref=landing,
                send_sem=sends.at[part, head],
                recv_sem=arrivals.at[part, head, piece],
                device_id=device(*there),
                device_id_type=MESH,
            ).start()
        pltpu.make_async_copy(
            source[part].at[pl.ds(taken, count), columns(mine, head)], landing, arrivals.at[part, head, piece]
        ).start()

    def shift(number):
        strip = pl.ds(number * (rows // 8), rows // 8)
        return pltpu.make_async_remote_copy(
            src_ref=resid.at[strip],
            dst_ref=inc.at[strip],
            send_sem=shifts.at[0],
            recv_sem=shifts.at[1],
            device_id=following,
            device_id_type=MESH,
        )

    quarter = rows // 4

    starts, sizes = ((0, 1, 3, 6), (1, 2, 3, 2))
    eighth = rows // 8

    def strip_of(number):
        return pl.ds(starts[number] * eighth, sizes[number] * eighth)

    def carried(number):
        return via.at[pl.ds(0, sizes[number] * eighth)]

    def detour(number):
        taken = resid.at[strip_of(number)]
        return pltpu.make_async_remote_copy(
            src_ref=taken,
            dst_ref=inc.at[strip_of(0)] if number == 0 else carried(number),
            send_sem=shifts.at[0],
            recv_sem=shifts.at[1] if number == 0 else detours.at[0],
            device_id={"section": 4 + number},
            device_id_type=MESH,
        )

    def forward(number):
        return pltpu.make_async_remote_copy(
            src_ref=carried(number),
            dst_ref=inc.at[strip_of(number)],
            send_sem=detours.at[1],
            recv_sem=shifts.at[1],
            device_id={"section": 4},
            device_id_type=MESH,
        )

    shared = functools.reduce(jnp.logical_or, [section == node for node in (0, 4, 5)])

    def send_resid(numbers, where):
        @pl.when(jnp.logical_and(where, jnp.logical_and(section < 7, section != 3)))
        def _():
            for number in numbers:
                shift(number).start()

    def send_detour(number):
        @pl.when(section == 3)
        def _():
            detour(number).start()

    def forward_detours():
        for number in range(1, 4):

            @pl.when(section == 4 + number)
            def _():
                settle(carried(number), detours.at[0])
                forward(number).start()

    is_last = section == 7

    send_resid(range(EARLY), section >= 0)

    @pl.when(is_last)
    def _():
        for part, head in ((K, 0), (V, 0), (K, 1)):
            spread(part, head)

    @pl.when(jnp.logical_not(is_last))
    def _():
        for part in (K, V, Q):
            spread(part, 0)

    send_resid(range(EARLY, 8), jnp.logical_not(shared))

    def fill(tile, carry):
        lanes = [jnp.full((1, TILE), mask[u, tile], jnp.int32) for u in range(span // TILE)]
        allowed = jnp.concatenate(lanes, axis=1)
        bias[tile] = jnp.where(allowed > 0, 0.0, LOW)

        @pl.when(jnp.logical_and(is_last, tile < span // TILE))
        def _():
            again = [jnp.full((1, TILE), mask[u, tile + span // TILE], jnp.int32) for u in range(span // TILE)]
            times = allowed + jnp.concatenate(again, axis=1)
            bias[tile] = jnp.where(times > 1, 1.0 / RATE, jnp.where(times > 0, 0.0, LOW))

        return carry

    lax.fori_loop(0, 3 * span // TILE, fill, 0)
    for copy, held, picked in zip(caches, (all_ck, all_cv), (ck, cv)):
        copy.wait()
        for i in range(4):
            picked[pl.ds(i * quarter, quarter), :] = held[chosen[0], pl.ds(i * quarter, quarter), :]

    def spread_cached(part, head):
        for sub in range(2):
            spread(part, head, sub)

    @pl.when(section == 0)
    def _():
        inc[...] = jnp.zeros_like(inc)

    top[...] = jnp.full_like(top, LOW / 2)
    total[...] = jnp.zeros_like(total)
    acc[...] = jnp.zeros_like(acc)

    def settle(ref, sem):
        pltpu.make_async_copy(ref, ref, sem).wait()

    def arrived(part, head, piece):
        buffer, first = home[part]
        settle(buffer.at[head, pl.ds(first + piece * part_rows, part_rows)], arrivals.at[part, head, piece])

    def cached_arrived(part, head, sub):
        buffer, first = home[part]
        settle(buffer.at[head, pl.ds(first + sub * block, block)], arrivals.at[part, head, sub])

    def all_arrived(part, head):
        for piece in range(PIECES):
            arrived(part, head, piece)

    def stream(tree):
        return kb if tree == 0 else vb

    def fresh_arrived(tree, head, piece):
        block_ref = stream(tree).at[head, pl.ds(span + piece * part_rows, part_rows)]
        settle(block_ref, fresh.at[tree, head, piece])

    def pass_on(tree, head, piece, first, slot, target):
        return pltpu.make_async_remote_copy(
            src_ref=stream(tree).at[head, pl.ds(first + piece * part_rows, part_rows)],
            dst_ref=stream(tree).at[head, pl.ds(span + piece * part_rows, part_rows)],
            send_sem=relay_sends.at[tree, head, piece, slot],
            recv_sem=fresh.at[tree, head, piece],
            device_id=near[target],
            device_id_type=MESH,
        )

    def relay(tree, head, piece, nodes=(0, 3, 4, 5, 6)):
        for node, targets in TREES[tree].items():
            if node not in nodes:
                continue

            @pl.when(section == node)
            def _():
                fresh_arrived(tree, head, piece)
                for slot, target in enumerate(targets):
                    pass_on(tree, head, piece, span, slot, target).start()

    def leaf(tree):
        inner = [section != node for node in TREES[tree]]
        return functools.reduce(jnp.logical_and, inner)

    def take_fresh(tree, head, pieces):
        @pl.when(leaf(tree))
        def _():
            for piece in pieces:
                fresh_arrived(tree, head, piece)

    def do(action, *args):
        return functools.partial(action, *args)

    @pl.when(is_last)
    def _():
        following_sends = iter((do(spread, V, 1), do(spread, Q, 0), do(spread, Q, 1), do(spread_cached, CK, 0)))
        for head in range(2):
            for tree, part in ((0, K), (1, V)):
                for piece in range(PIECES):
                    arrived(part, head, piece)
                    for slot, target in enumerate(TREES[tree][7]):
                        pass_on(tree, head, piece, 0, slot, target).start()
                next(following_sends)()
        all_arrived(Q, 0)
        spread_cached(CV, 0)

    @pl.when(jnp.logical_not(is_last))
    def _():
        all_arrived(K, 0)
        spread_cached(CK, 0)
        for piece in range(2):
            relay(0, 0, piece, (4,))
        all_arrived(V, 0)
        spread_cached(CV, 0)
        for piece in range(2, 4):
            relay(0, 0, piece, (4,))
        all_arrived(Q, 0)
        spread(Q, 1)

    def tail(first):
        return {
            (first - 1, 1): [do(cached_arrived, CK, 1, 0)],
            (first, 0): [do(cached_arrived, CV, 1, 0)],
            (first, 1): [do(cached_arrived, CK, 1, 1)],
            (first + 1, 0): [do(cached_arrived, CV, 1, 1), forward_detours],
        }

    others = {
        (0, 0): [do(relay, 1, 0, 0), do(relay, 0, 0, 0, (0, 5))],
        (0, 1): [do(relay, 1, 0, 1), do(relay, 0, 0, 1, (0, 5))],
        (1, 0): [do(relay, 1, 0, 2), do(relay, 0, 0, 2, (0, 5)), do(relay, 0, 0, 0, (3,))],
        (1, 1): [do(relay, 1, 0, 3), do(relay, 0, 0, 3, (0, 5))]
        + [do(relay, 0, 0, p, (3,)) for p in (1, 2, 3)]
        + [do(relay, 0, 1, p, (4,)) for p in range(4)]
        + [do(cached_arrived, CK, 0, 0), do(spread, K, 1)],
        (2, 0): [do(cached_arrived, CV, 0, 0), do(relay, 1, 1, 0, (6, 3)), do(relay, 0, 1, 0, (0, 5))],
        (2, 1): [
            do(spread, V, 1),
            do(cached_arrived, CK, 0, 1),
            do(relay, 1, 1, 1, (6, 3)),
            do(relay, 0, 1, 1, (0, 5)),
        ],
        (3, 0): [
            do(cached_arrived, CV, 0, 1),
            do(relay, 1, 1, 2, (6, 3)),
            do(relay, 0, 1, 2, (0, 5)),
            do(relay, 1, 1, 0, (5,)),
            do(relay, 0, 1, 0, (3,)),
        ],
        (3, 1): [
            do(spread_cached, CK, 1),
            do(send_resid, (3, 4), shared),
            do(relay, 1, 1, 3, (6, 3)),
            do(relay, 0, 1, 3, (0, 5)),
            do(relay, 1, 1, 1, (5,)),
            do(relay, 0, 1, 1, (3,)),
            do(take_fresh, 0, 0, (0, 1)),
        ],
        (4, 0): [
            do(send_resid, (5,), shared),
            do(take_fresh, 1, 0, (0, 1)),
            do(relay, 1, 1, 2, (5,)),
            do(relay, 0, 1, 2, (3,)),
        ],
        (4, 1): [
            do(take_fresh, 0, 0, (2, 3)),
            do(relay, 1, 1, 3, (5,)),
            do(relay, 0, 1, 3, (3,)),
            do(spread_cached, CV, 1),
            do(send_resid, (6, 7), shared),
        ],
        (5, 0): [do(take_fresh, 1, 0, (2, 3))],
        (5, 1): [do(all_arrived, Q, 1), do(take_fresh, 0, 1, (0, 1))],
        (6, 0): [do(send_detour, 1), do(take_fresh, 1, 1, (0, 1))],
        (6, 1): [do(take_fresh, 0, 1, (2, 3))],
        (7, 0): [do(send_detour, 2), do(take_fresh, 1, 1, (2, 3))],
        (7, 1): [do(all_arrived, K, 1)],
        (8, 0): [do(send_detour, 3), do(all_arrived, V, 1)],
        (9, 0): [do(send_detour, 0)],
        **tail(10),
    }
    last = {
        (1, 1): [do(all_arrived, Q, 1), do(spread_cached, CK, 1)],
        (2, 1): [do(spread_cached, CV, 1)],
        (3, 1): [do(cached_arrived, CK, 0, 0)],
        (4, 0): [do(cached_arrived, CV, 0, 0)],
        (4, 1): [do(cached_arrived, CK, 0, 1)],
        (5, 0): [do(cached_arrived, CV, 0, 1)],
        **tail(6),
    }

    def point(stage, at):
        for wanted, table in ((is_last, last), (jnp.logical_not(is_last), others)):
            for (number, where), actions in table.items():
                if where == at:

                    @pl.when(jnp.logical_and(stage == number, wanted))
                    def _():
                        for action in actions:
                            action()

    tiles = block // TILE

    def locate(stage):
        pair = stage // 2
        head = jnp.where(is_last, lax.rem(pair, 2), pair // 3)
        kind_others = jnp.where(pair < 3, lax.rem(2 * pair, 3), lax.rem(2 * pair + 1, 3))
        kind = jnp.where(is_last, 2 * (pair // 2), kind_others)
        cached = kind == 2
        index = 2 * kind + lax.rem(stage, 2)
        first = jnp.where(cached, 4 * tiles + lax.rem(stage, 2), index * tiles)
        return head, (first, jnp.where(cached, 2, 1)), pl.ds(pl.multiple_of(index * block, block), block)

    def half_rows(half):
        return pl.ds(pl.multiple_of(half * block, block), block)

    def score(stage, half, out):
        head, _, keys = locate(stage)
        out[...] = lax.dot_general(
            kb[head, keys, :],
            qb[head, half_rows(half), :],
            (((1,), (1,)), ((), ())),
            preferred_element_type=F32,
        )

    def absorb(stage, half, scores):
        head, (first, pace), keys = locate(stage)
        biases = [bias[first + t * pace, :, half_rows(half)] for t in range(tiles)]
        old = top[head, half]
        new = old
        for t in range(tiles):
            new = jnp.maximum(new, jnp.max(scores[pl.ds(t * TILE, TILE), :], axis=0, keepdims=True) + biases[t])
        top[head, half] = new
        factor = jnp.exp2((old - new) * RATE)
        expo = [
            jnp.exp2((scores[pl.ds(t * TILE, TILE), :] - (new - biases[t])) * RATE) for t in range(tiles)
        ]
        summed = total[head, half] * factor
        for part in expo:
            summed = summed + jnp.sum(part, axis=0, keepdims=True)
        total[head, half] = summed
        weight = jnp.concatenate([part.astype(BF16) for part in expo], axis=0)
        acc[head, half] = acc[head, half] * factor + lax.dot_general(
            vb[head, keys, :], weight, (((0,), (0,)), ((), ())), preferred_element_type=F32
        )

    def result(head):
        return attn.at[:, columns(mine, head)]

    def finish(head, half):
        ob[head, half_rows(half), :] = (acc[head, half] / total[head, half]).T.astype(BF16)
        for step in OTHERS:
            there = other(step)

            @pl.when(there[2] // 2 == half)
            def _():
                owner = there[2] * 2 + there[3]
                pltpu.make_async_remote_copy(
                    src_ref=ob.at[head, pl.ds(pl.multiple_of(owner * rows, rows), rows)],
                    dst_ref=result(head),
                    send_sem=out_sends.at[head],
                    recv_sem=out_arrivals.at[head],
                    device_id=device(*there),
                    device_id_type=MESH,
                ).start()

        @pl.when(x // 2 == half)
        def _():
            pltpu.make_async_copy(
                ob.at[head, pl.ds(pl.multiple_of(seq * rows, rows), rows)], result(head), out_arrivals.at[head]
            ).start()

    far = 1 - x // 2
    stages = jnp.where(is_last, 8, 12)
    score(0, far, score_a)

    def stage_body(stage, carry):
        head = stage // (stages - 1)
        ends = jnp.logical_or(stage == 5, stage == stages - 1)
        point(stage, 0)
        score(stage, 1 - far, score_b)
        absorb(stage, far, score_a)

        @pl.when(ends)
        def _():
            finish(head, far)

        point(stage, 1)
        score(jnp.minimum(stage + 1, stages - 1), far, score_a)
        absorb(stage, 1 - far, score_b)

        @pl.when(ends)
        def _():
            finish(head, 1 - far)

        return carry

    lax.fori_loop(0, stages, stage_body, 0)

    for tree in range(2):
        for node, targets in TREES[tree].items():

            @pl.when(section == node)
            def _():
                for head in range(2):
                    for piece in range(PIECES):
                        for slot, target in enumerate(targets):
                            pass_on(tree, head, piece, span, slot, target).wait_send()

    @pl.when(section < 7)
    def _():
        settle(resid, shifts.at[0])

    for number in range(1, 4):

        @pl.when(section == 4 + number)
        def _():
            settle(carried(number), detours.at[1])

    @pl.when(section > 0)
    def _():
        settle(inc, shifts.at[1])

    for head in range(2):
        for part in range(5):
            settle(home[part][0].at[head, pl.ds(0, 7 * rows)], sends.at[part, head])
        settle(ob.at[head, pl.ds(0, 7 * rows)], out_sends.at[head])
        settle(ob.at[head], out_arrivals.at[head])
    out[...] = (inc[...].astype(F32) + attn[...].astype(F32)).astype(BF16)


def fused(q, k, v, cache_k, cache_v, resid, chosen, mask):
    rows, width = q.shape
    span = rows * 8
    half = span // 2
    dma = pltpu.SemaphoreType.DMA
    smem = pl.BlockSpec(memory_space=pltpu.SMEM)
    return pl.pallas_call(
        functools.partial(fused_kernel, span),
        out_shape=jax.ShapeDtypeStruct((rows, width), BF16),
        in_specs=[HBM] * 6 + [smem] * 2,
        out_specs=VMEM,
        scratch_shapes=[
            pltpu.VMEM((2, span, HD), BF16),
            pltpu.VMEM((2, 3 * span, HD), BF16),
            pltpu.VMEM((2, 3 * span, HD), BF16),
            pltpu.VMEM((2, span, HD), BF16),
            pltpu.VMEM((half, half), F32),
            pltpu.VMEM((half, half), F32),
            pltpu.VMEM((2, 2, 1, half), F32),
            pltpu.VMEM((2, 2, 1, half), F32),
            pltpu.VMEM((2, 2, HD, half), F32),
            pltpu.VMEM((3 * span // TILE, 1, span), F32),
            pltpu.VMEM(cache_k.shape, BF16),
            pltpu.VMEM(cache_v.shape, BF16),
            pltpu.VMEM((rows, width), BF16),
            pltpu.VMEM((rows, width), BF16),
            pltpu.VMEM((rows, width), BF16),
            pltpu.VMEM((rows, width), BF16),
            pltpu.VMEM((3 * rows // 8, width), BF16),
            dma((5, 2)),
            dma((5, 2, PIECES)),
            dma((2,)),
            dma((2, 2, PIECES)),
            dma((2, 2, PIECES, 2)),
            dma((2,)),
            dma((2,)),
            dma((2,)),
            dma((2,)),
        ],
        name="fused",
        compiler_params=pltpu.CompilerParams(
            collective_id=0, has_side_effects=True, vmem_limit_bytes=60 * 2**20
        ),
    )(q, k, v, cache_k, cache_v, resid, chosen, mask)


def body(resid, span_q, span_k, span_v, cache_k, cache_v, cache_index, tile_mask):
    return fused(
        span_q[0], span_k[0], span_v[0], cache_k, cache_v, resid[0], cache_index, tile_mask[0]
    )[None]


def solution(mesh):
    placed = (
        P("section", "seq", "mp"),
        P("section", "seq", "mp"),
        P("section", "seq", "mp"),
        P("section", "seq", "mp"),
        P(None, "seq", "mp"),
        P(None, "seq", "mp"),
        P("section"),
        P("section", None, None),
    )
    return jax.shard_map(
        body, mesh=mesh, in_specs=placed, out_specs=P("section", "seq", "mp"), check_vma=False
    )
```
